128 devices in a mesh: vocab: 32 (over z, x, core), tp: 4 (over y).
Axes of the slice: x: 4, y: 4, z: 4, core: 2. Of those that a mesh axis runs over, the one named last changes fastest.
Arguments:
- hidden: bfloat16 [16384, 2048], P('vocab'), may hold values from -28 to 28, as said below
- target_cluster: int32 [16384, 1], P('vocab'), may hold values from 0 to 255; in each aligned block of 512 rows (0 to 511, 512 to 1023, ...) at most 4 rows name the same one
- target_word: int32 [16384], P('vocab'), may hold values from 0 to 8191
- head_words: bfloat16 [2048, 8192], P(None, 'tp'), may hold values from -4 to 4
- head_clusters: bfloat16 [2048, 128], P(None, 'tp'), may hold values from -4 to 4
- proj_one: bfloat16 [32, 2048, 1024], P('vocab'), may hold values from -0.125 to 0.125
- proj_two: bfloat16 [32, 2048, 512], P('vocab'), may hold values from -0.125 to 0.125
- proj_three: bfloat16 [32, 2048, 256], P('vocab'), may hold values from -0.125 to 0.125
- proj_four: bfloat16 [32, 2048, 128], P('vocab'), may hold values from -0.125 to 0.125
- out_one: bfloat16 [32, 1024, 1024], P('vocab', None, 'tp'), may hold values from -4 to 4
- out_two: bfloat16 [32, 512, 2048], P('vocab', None, 'tp'), may hold values from -4 to 4
- out_three: bfloat16 [32, 256, 4096], P('vocab', None, 'tp'), may hold values from -4 to 4
- out_four: bfloat16 [32, 128, 8192], P('vocab', None, 'tp'), may hold values from -4 to 4
Outputs:
- grad_hidden: bfloat16 [16384, 2048], P('vocab', 'tp')
- grad_head_words: bfloat16 [2048, 8192], P('vocab', 'tp')
- grad_head_clusters: bfloat16 [2048, 128], P('vocab', 'tp')
- grad_proj_one: bfloat16 [32, 2048, 1024], P('vocab', 'tp')
- grad_proj_two: bfloat16 [32, 2048, 512], P('vocab', 'tp')
- grad_proj_three: bfloat16 [32, 2048, 256], P('vocab', 'tp')
- grad_proj_four: bfloat16 [32, 2048, 128], P('vocab', 'tp')
- grad_out_one: bfloat16 [32, 1024, 1024], P('vocab', None, 'tp')
- grad_out_two: bfloat16 [32, 512, 2048], P('vocab', None, 'tp')
- grad_out_three: bfloat16 [32, 256, 4096], P('vocab', None, 'tp')
- grad_out_four: bfloat16 [32, 128, 8192], P('vocab', None, 'tp')
The draws below stay inside these ranges and needn't reach their ends.
Inputs may be any that keep to these rules, and one draw needn't show every extreme that they name: `hidden`: real values of order one, up to a factor that differs between tokens. `target_cluster`: A value below 128 names the tail cluster of the token's word; 128 or more marks a word of the head. Among the 512 tokens of one index of vocab no tail cluster is named more than 4 times. `target_word`: for a tail token only the value modulo its cluster's vocabulary counts.
All inputs are finite; a program needn't handle non-finite values.
Results may differ from the reference program's by a relative error of at most 0.017.
Values may be sent and summed in bfloat16 or wider, within the bound.
A program may use at most 128 MiB of HBM per device.

```python
import math
import jax
import jax.numpy as jnp
import numpy as np
from jax import lax

D = 2048
HEAD_WORDS = 8192
D1 = 1024
D2 = 512
D3 = 256
D4 = 128
VOC1 = 1024
VOC2 = 2048
VOC3 = 4096
VOC4 = 8192
TOK_DEV = 512
CL_BAND = 32
CLUSTERS = 128
CAP = 4
TOKENS = 16384
N_VOCAB = 32


def draw_hidden(key, part):
    first, second = jax.random.split(key)
    scales = jnp.exp(jax.random.uniform(second, (TOKENS, 1), jnp.float32, jnp.log(0.25), jnp.log(4.0)))
    values = jnp.clip(jax.random.normal(first, (TOKENS, D), jnp.float32), -6.0, 6.0) * scales
    return values.astype(jnp.bfloat16)


def head_offset(key):
    return jax.random.uniform(jax.random.fold_in(key, 7001), (D, 1), jnp.float32, -0.3, 0.3)


def band_offset(key, salt_value, width):
    return jax.random.uniform(jax.random.fold_in(key, salt_value), (CL_BAND, width, 1), jnp.float32, -0.3, 0.3)


def shifted(key, salt_value, shape, fan_in, offset):
    values = jnp.clip(jax.random.normal(jax.random.fold_in(key, salt_value), shape, jnp.float32), -3.0, 3.0)
    return values * (16.0 / fan_in) ** 0.5 + offset


def draw_head_words(key, part):
    return shifted(key, 7002, (D, HEAD_WORDS), D, head_offset(key)).astype(jnp.bfloat16)


def draw_head_clusters(key, part):
    return shifted(key, 7003, (D, CLUSTERS), D, head_offset(key)).astype(jnp.bfloat16)


def draw_out_one(key, part):
    return shifted(key, 7201, (CL_BAND, D1, VOC1), D1, band_offset(key, 7101, D1)).astype(jnp.bfloat16)


def draw_out_two(key, part):
    return shifted(key, 7202, (CL_BAND, D2, VOC2), D2, band_offset(key, 7102, D2)).astype(jnp.bfloat16)


def draw_out_three(key, part):
    return shifted(key, 7203, (CL_BAND, D3, VOC3), D3, band_offset(key, 7103, D3)).astype(jnp.bfloat16)


def draw_out_four(key, part):
    return shifted(key, 7204, (CL_BAND, D4, VOC4), D4, band_offset(key, 7104, D4)).astype(jnp.bfloat16)


def place_ends(drawn, rng, least, top_value):
    index_at = [jax.random.randint(jax.random.fold_in(rng, axis), (), 0, length) for axis, length in enumerate(drawn.shape)]
    widest = drawn.shape.index(max(drawn.shape))
    beside = index_at[:widest] + [(index_at[widest] + 1) % drawn.shape[widest]] + index_at[widest + 1:]
    return drawn.at[tuple(index_at)].set(least).at[tuple(beside)].set(top_value)


def levels(rng, dims, cuts, least, largest):
    def one(axis_at, blocks):
        heights = jax.random.uniform(jax.random.fold_in(jax.random.fold_in(rng, 6), axis_at), (blocks,), jnp.float32, least / len(cuts), largest / len(cuts))
        return jnp.repeat(jnp.exp(heights), dims[axis_at] // blocks).reshape((-1,) + (1,) * (len(dims) - axis_at - 1))

    level = one(*cuts[0])
    for cut in cuts[1:]:
        level = level * one(*cut)
    return level


def cumulative_ranks(count, slope):
    weights = [(1 << 20) // math.isqrt(rank ** slope) + 1 for rank in range(1, count + 1)]
    scale = 1 + sum(weights) // (1 << 30)
    return np.cumsum(np.array([max(1, weight // scale) for weight in weights]))


def ranked_ids(own_key, shape, count, skew):
    grid = cumulative_ranks(count, skew)
    ticket = jax.random.randint(jax.random.fold_in(own_key, 1), shape, 0, int(grid[count - 1]))
    grade = jnp.searchsorted(jnp.asarray(grid, jnp.int32), ticket, side="right")
    return jax.random.permutation(jax.random.fold_in(own_key, 2), count)[grade].astype(jnp.int32)


def routed_block(key, own, number, rows, number_of, top, most, slope):
    ranking = jax.random.permutation(key, number_of)
    packed, ordinary = load_shares(number_of, rows * top, most, slope, True), load_shares(number_of, rows * top, most, slope, False)
    places = jnp.arange(number_of)

    def named(tallies, offset_by):
        used = int((tallies > 0).sum())
        fixed = max(1, used // 4)
        passed = fixed + (places - fixed + offset_by * (used - fixed)) % max(1, number_of - fixed)
        return jnp.zeros((number_of,), jnp.int32).at[ranking[jnp.where(places < fixed, places, passed)]].set(jnp.asarray(tallies, jnp.int32))

    tallies = jnp.where(number % 4 == 0, named(packed, number // 4), named(ordinary, number - number // 4 - 1))
    mixed = jax.random.permutation(jax.random.fold_in(own, 3), number_of)
    giver, receiver = mixed[0:number_of // 2 * 2:2], mixed[1:number_of // 2 * 2:2]
    slack = jnp.minimum(tallies[giver] - 1, most - tallies[receiver]) // 2
    slack = jnp.where((giver == ranking[0]) | (receiver == ranking[0]) | (tallies[receiver] == 0), 0, jnp.maximum(slack, 0))
    passed = jax.random.randint(jax.random.fold_in(own, 4), (number_of // 2,), 0, 1 << 20) % (slack + 1)
    tallies = tallies.at[giver].add(-passed).at[receiver].add(passed)
    items = jnp.searchsorted(jnp.cumsum(tallies), jnp.arange(rows * top), side="right").astype(jnp.int32)
    grid = items.reshape(top, rows).T
    grid = grid[jax.random.permutation(jax.random.fold_in(own, 1), rows)]
    offset_by = jax.random.randint(jax.random.fold_in(own, 2), (rows, 1), 0, top)
    return jnp.take_along_axis(grid, (jnp.arange(top)[None, :] + offset_by) % top, axis=1)


def load_shares(count, total, most, skew, full):
    portions = [(1 << 20) // math.isqrt(grade ** skew) + 1 for grade in range(1, count + 1)]
    largest = most if full else min(most, max(-(-total // count), total * portions[0] // sum(portions)))
    least = 1 if total - largest >= count - 1 else 0
    given, surplus = [largest] + [least] * (count - 1), total - largest - least * (count - 1)
    while surplus > 0:
        free = [i for i in range(1, count) if given[i] < largest] or [i for i in range(1, count) if given[i] < most]
        pool, left = sum([portions[i] for i in free]), surplus
        for i in free:
            addition = min(most - given[i], max(1, left * portions[i] // pool), surplus)
            given[i] = given[i] + addition
            surplus = surplus - addition
    return np.array(given)


def noise(stream_key, extent, spread, limit, pieces=(), kind=jnp.bfloat16):
    entries = spread * jax.random.normal(stream_key, extent, jnp.float32)
    if pieces:
        entries = entries * levels(stream_key, extent, pieces, -0.22, 0.18)
    return jnp.clip(entries, -limit, limit).astype(kind)


def setup_inputs(seed: int = 0) -> dict:
    splits = jax.random.split(jax.random.key(seed), 14)
    hidden = draw_hidden(jax.random.fold_in(splits[13], 71), 0)
    target_cluster_keys = jax.random.split(jax.random.fold_in(splits[1], 1), TOKENS // TOK_DEV)
    target_cluster_turns = jax.random.permutation(jax.random.fold_in(splits[1], 3), TOKENS // TOK_DEV)
    target_cluster = jax.vmap(lambda own, number: routed_block(jax.random.fold_in(splits[1], 2), own, number, TOK_DEV, 2 * CLUSTERS, 1, CAP, 2))(target_cluster_keys, target_cluster_turns).reshape((TOKENS, 1))
    target_word = place_ends(ranked_ids(splits[2], (TOKENS,), HEAD_WORDS, 1), jax.random.fold_in(splits[2], 3), 0, HEAD_WORDS - 1).astype(jnp.int32)
    head_words = draw_head_words(jax.random.fold_in(splits[13], 71), 0)
    head_clusters = draw_head_clusters(jax.random.fold_in(splits[13], 71), 0)
    proj_one = noise(splits[5], (CL_BAND, D, D1), D ** -0.5, 0.125, ((0, 32),))
    proj_two = noise(splits[6], (CL_BAND, D, D2), D ** -0.5, 0.125, ((0, 32),))
    proj_three = noise(splits[7], (CL_BAND, D, D3), D ** -0.5, 0.125, ((0, 32),))
    proj_four = noise(splits[8], (CL_BAND, D, D4), D ** -0.5, 0.125, ((0, 32),))
    out_one = draw_out_one(jax.random.fold_in(splits[13], 71), 0)
    out_two = draw_out_two(jax.random.fold_in(splits[13], 71), 0)
    out_three = draw_out_three(jax.random.fold_in(splits[13], 71), 0)
    out_four = draw_out_four(jax.random.fold_in(splits[13], 71), 0)
    return {"hidden": hidden, "target_cluster": target_cluster, "target_word": target_word, "head_words": head_words, "head_clusters": head_clusters, "proj_one": proj_one, "proj_two": proj_two, "proj_three": proj_three, "proj_four": proj_four, "out_one": out_one, "out_two": out_two, "out_three": out_three, "out_four": out_four}


def head_pass(hidden, head_col, weights):
    cols = weights.shape[1]
    blocks_rows = hidden.reshape(-1, TOK_DEV, D)
    blocks_cols = head_col.reshape(-1, TOK_DEV)

    def step(carry, inputs):
        rows, target = inputs
        logits = jnp.dot(rows, weights, preferred_element_type=jnp.float32)
        peak = jnp.max(logits, axis=1, keepdims=True)
        expd = jnp.exp(logits - peak)
        probs = expd / jnp.sum(expd, axis=1, keepdims=True)
        hit = (jnp.arange(cols, dtype=jnp.int32)[None, :] == target[:, None]).astype(jnp.float32)
        grads = (probs - hit).astype(jnp.bfloat16)
        back = jnp.dot(grads, weights.T, preferred_element_type=jnp.float32)
        return carry + jnp.dot(rows.T, grads, preferred_element_type=jnp.float32), back

    init = jnp.zeros((D, cols), jnp.float32)
    total, backs = lax.scan(step, init, (blocks_rows, blocks_cols))
    return total, backs.reshape(-1, D)


def band_pass(rows, words, proj, outw, vocab):
    def one(args):
        block, word, weight_in, weight_out = args
        valid = word >= 0
        local = jnp.where(valid, word % vocab, -1)
        reduced = jnp.dot(block, weight_in, preferred_element_type=jnp.float32).astype(jnp.bfloat16)
        logits = jnp.dot(reduced, weight_out, preferred_element_type=jnp.float32)
        peak = jnp.max(logits, axis=1, keepdims=True)
        expd = jnp.exp(logits - peak)
        probs = expd / jnp.sum(expd, axis=1, keepdims=True)
        hit = (jnp.arange(vocab, dtype=jnp.int32)[None, :] == local[:, None]).astype(jnp.float32)
        dlog = ((probs - hit) * valid[:, None].astype(jnp.float32)).astype(jnp.bfloat16)
        dred = jnp.dot(dlog, weight_out.T, preferred_element_type=jnp.float32).astype(jnp.bfloat16)
        grad_out = jnp.dot(reduced.T, dlog, preferred_element_type=jnp.float32).astype(jnp.bfloat16)
        grad_proj = jnp.dot(block.T, dred, preferred_element_type=jnp.float32).astype(jnp.bfloat16)
        back = jnp.dot(dred, weight_in.T, preferred_element_type=jnp.float32).astype(jnp.bfloat16)
        return grad_out, grad_proj, back

    return lax.map(one, (rows, words, proj, outw))


def reference(hidden, target_cluster, target_word, head_words, head_clusters, proj_one, proj_two, proj_three, proj_four, out_one, out_two, out_three, out_four):
    clus = target_cluster[:, 0]
    tail = clus < CLUSTERS
    head_col = jnp.where(tail, HEAD_WORDS + clus, target_word).astype(jnp.int32)
    weights = jnp.concatenate([head_words, head_clusters], axis=1)
    head_total, head_back = head_pass(hidden, head_col, weights)

    tok_index = jnp.arange(TOKENS, dtype=jnp.int32)
    member = (clus.reshape(N_VOCAB, TOK_DEV)[:, :, None] == jnp.arange(CLUSTERS, dtype=jnp.int32)[None, None, :]).astype(jnp.int32)
    rank = jnp.sum((jnp.cumsum(member, axis=1) - 1) * member, axis=2).reshape(TOKENS)
    source = tok_index // TOK_DEV
    row_key = jnp.where(tail, clus, CLUSTERS).astype(jnp.int32)
    slot = (source * CAP + rank).astype(jnp.int32)
    table = jnp.full((CLUSTERS, N_VOCAB * CAP), TOKENS, jnp.int32).at[row_key, slot].set(tok_index, mode="drop")
    hidden_pad = jnp.concatenate([hidden, jnp.zeros((1, D), jnp.bfloat16)], axis=0)
    word_pad = jnp.concatenate([target_word, jnp.full((1,), -1, jnp.int32)], axis=0)

    tail_back = jnp.zeros((TOKENS + 1, D), jnp.float32)
    grads_out = []
    grads_proj = []
    bands = ((proj_one, out_one, VOC1), (proj_two, out_two, VOC2), (proj_three, out_three, VOC3), (proj_four, out_four, VOC4))
    for band, (proj, outw, vocab) in enumerate(bands):
        table_band = table[band * CL_BAND:(band + 1) * CL_BAND]
        rows = hidden_pad[table_band]
        words = word_pad[table_band]
        grad_out, grad_proj, back = band_pass(rows, words, proj, outw, vocab)
        tail_back = tail_back.at[table_band.reshape(-1)].add(back.reshape(-1, D).astype(jnp.float32))
        grads_out.append(grad_out)
        grads_proj.append(grad_proj)

    grad_hidden = (head_back + tail_back[:TOKENS]).astype(jnp.bfloat16)
    grad_head_words = head_total[:, :HEAD_WORDS].astype(jnp.bfloat16)
    grad_head_clusters = head_total[:, HEAD_WORDS:].astype(jnp.bfloat16)
    return (grad_hidden, grad_head_words, grad_head_clusters, grads_proj[0], grads_proj[1], grads_proj[2], grads_proj[3], grads_out[0], grads_out[1], grads_out[2], grads_out[3])
```

```python
import jax
import jax.numpy as jnp
from jax import lax
from jax.sharding import PartitionSpec as P


def sent_to_all(array, axis):
    copies = jnp.broadcast_to(array, (lax.axis_size(axis), *array.shape))
    return lax.all_to_all(copies, axis, split_axis=0, concat_axis=0, tiled=True)


def gathered_once(array, axis):
    leaves = jax.tree.leaves(array)
    order = sorted(range(len(leaves)), key=lambda k: -leaves[k].size)
    width = (1, *leaves[order[0]].shape)[-1]
    lines = [
        jnp.pad(leaves[k].reshape(-1), (0, -leaves[k].size % width)).reshape(-1, width)
        for k in order
    ]
    both, at, found = (sent_to_all(jnp.concatenate(lines), axis), 0, {})
    for k, line in zip(order, lines):
        share = both[:, at : at + len(line)].reshape(len(both), -1)
        found[k] = share[:, : leaves[k].size].reshape(-1, *leaves[k].shape)
        at += len(line)
    numbers = iter(range(len(leaves)))
    return jax.tree.map(lambda _: found[next(numbers)], array)


def combined_pairwise(pieces, combine):
    while len(jax.tree.leaves(pieces)[0]) > 1:
        pieces = jax.vmap(combine)(
            *(jax.tree.map(lambda part: part[side::2], pieces) for side in (0, 1))
        )
    return jax.tree.map(lambda part: part[0], pieces)


def merged(array, axis, combine):
    pieces = gathered_once(array, axis)
    return combined_pairwise(pieces, combine)


def split_up(array, dim, length):
    lengths = array.shape
    parts = array.reshape(*lengths[:dim], length, lengths[dim] // length, *lengths[dim + 1 :])
    return jnp.moveaxis(parts, dim, 0)


def sum_at_owner(array, axis, dim):
    parts = split_up(array, dim, lax.axis_size(axis))
    arrived = lax.all_to_all(parts, axis, split_axis=0, concat_axis=0, tiled=True)
    return arrived.astype(jnp.float32).sum(axis=0)


def of_everyone(array, axis):
    return sent_to_all(array, axis).astype(jnp.float32).sum(axis=0)


def online_pair(first, second):
    head_peak = jnp.maximum(first[0], second[0])
    head_total = first[1] * jnp.exp(first[0] - head_peak) + second[1] * jnp.exp(
        second[0] - head_peak
    )
    tail_peak = jnp.maximum(first[2], second[2])
    tail_total = first[3] * jnp.exp(first[2] - tail_peak) + second[3] * jnp.exp(
        second[2] - tail_peak
    )
    return (head_peak, head_total, tail_peak, tail_total)


def body(
    hidden,
    target_cluster,
    target_word,
    head_words,
    head_clusters,
    proj_one,
    proj_two,
    proj_three,
    proj_four,
    out_one,
    out_two,
    out_three,
    out_four,
):
    groups = lax.axis_size("vocab")
    splits = lax.axis_size("tp")
    tp_index = lax.axis_index("tp")
    tok_rows, width = hidden.shape
    capacity = tok_rows // (4 * groups)
    clusters = 4 * groups
    slots = groups * capacity
    word_cols = head_words.shape[1]
    clus_cols = head_clusters.shape[1]
    own_width = width // splits
    logit_words = jnp.dot(hidden, head_words, preferred_element_type=jnp.float32)
    logit_clus = jnp.dot(hidden, head_clusters, preferred_element_type=jnp.float32)
    head_peak = jnp.maximum(jnp.max(logit_words, axis=1), jnp.max(logit_clus, axis=1))
    head_total = jnp.sum(jnp.exp(logit_words - head_peak[:, None]), axis=1) + jnp.sum(
        jnp.exp(logit_clus - head_peak[:, None]), axis=1
    )
    cluster_ids = target_cluster[:, 0]
    tail_mask = cluster_ids < clusters
    band_ids = cluster_ids // groups
    owner_ids = cluster_ids % groups
    order = jnp.arange(tok_rows, dtype=jnp.int32)
    earlier = (cluster_ids[:, None] == cluster_ids[None, :]) & (order[:, None] > order[None, :])
    rank = jnp.sum(earlier.astype(jnp.int32), axis=1)
    flat = jnp.where(tail_mask, owner_ids * 4 * capacity + band_ids * capacity + rank, -1)
    dispatch = jnp.arange(tok_rows, dtype=jnp.int32)[:, None] == flat[None, :]
    dispatch_bf = dispatch.astype(jnp.bfloat16)
    send_rows = jnp.dot(dispatch_bf, hidden, preferred_element_type=jnp.float32).astype(
        jnp.bfloat16
    )
    send_words = jnp.sum(dispatch.astype(jnp.int32) * (target_word + 1)[None, :], axis=1) - 1
    recv_rows, recv_words = (
        lax.all_to_all(
            send_rows.reshape(groups, 4 * capacity, width),
            "vocab",
            split_axis=0,
            concat_axis=0,
            tiled=True,
        ),
        lax.all_to_all(
            send_words.reshape(groups, 4 * capacity),
            "vocab",
            split_axis=0,
            concat_axis=0,
            tiled=True,
        ),
    )
    projections = (proj_one, proj_two, proj_three, proj_four)
    outputs = (out_one, out_two, out_three, out_four)
    grouped = (order % slots) // capacity * (4 * capacity) + order // slots * capacity + order % capacity
    regroup = (grouped[:, None] == order[None, :]).astype(jnp.bfloat16)
    sorted_rows = jnp.dot(
        regroup, recv_rows.reshape(tok_rows, width), preferred_element_type=jnp.float32
    ).astype(jnp.bfloat16)
    band_rows = []
    band_valid = []
    band_local = []
    band_reduced = []
    band_logits = []
    for band in range(4):
        rows = sorted_rows[band * slots : (band + 1) * slots]
        words = recv_words[:, band * capacity : (band + 1) * capacity].reshape(slots)
        weight_out = outputs[band][0]
        vcols = weight_out.shape[1]
        valid = words >= 0
        local = jnp.where(valid, words % (vcols * splits) - tp_index * vcols, -1)
        reduced = jnp.dot(rows, projections[band][0], preferred_element_type=jnp.float32).astype(
            jnp.bfloat16
        )
        logits = jnp.dot(reduced, weight_out, preferred_element_type=jnp.float32)
        band_rows.append(rows)
        band_valid.append(valid)
        band_local.append(local)
        band_reduced.append(reduced)
        band_logits.append(logits)
    tail_peak = jnp.stack([jnp.max(logits, axis=1) for logits in band_logits])
    tail_total = jnp.stack(
        [
            jnp.sum(jnp.exp(band_logits[band] - tail_peak[band][:, None]), axis=1)
            for band in range(4)
        ]
    )
    head_peak, head_total, tail_peak, tail_total = merged(
        (head_peak, head_total, tail_peak, tail_total), "tp", online_pair
    )
    word_target = jnp.where(tail_mask, -1, target_word - tp_index * word_cols)
    clus_target = jnp.where(tail_mask, cluster_ids - tp_index * clus_cols, -1)
    inverse = 1.0 / head_total
    probs_words = jnp.exp(logit_words - head_peak[:, None]) * inverse[:, None]
    probs_clus = jnp.exp(logit_clus - head_peak[:, None]) * inverse[:, None]
    hit_words = (jnp.arange(word_cols, dtype=jnp.int32)[None, :] == word_target[:, None]).astype(
        jnp.float32
    )
    hit_clus = (jnp.arange(clus_cols, dtype=jnp.int32)[None, :] == clus_target[:, None]).astype(
        jnp.float32
    )
    grad_words = (probs_words - hit_words).astype(jnp.bfloat16)
    grad_clus = (probs_clus - hit_clus).astype(jnp.bfloat16)
    head_part = jnp.dot(grad_words, head_words.T, preferred_element_type=jnp.float32) + jnp.dot(
        grad_clus, head_clusters.T, preferred_element_type=jnp.float32
    )
    head_mine = sum_at_owner(head_part.astype(jnp.bfloat16), "tp", 1)
    band_dlog = []
    partials = []
    for band in range(4):
        weight_out = outputs[band][0]
        vcols = weight_out.shape[1]
        probs = jnp.exp(band_logits[band] - tail_peak[band][:, None]) / tail_total[band][:, None]
        hit = (jnp.arange(vcols, dtype=jnp.int32)[None, :] == band_local[band][:, None]).astype(
            jnp.float32
        )
        dlog = ((probs - hit) * band_valid[band][:, None].astype(jnp.float32)).astype(jnp.bfloat16)
        band_dlog.append(dlog)
        partials.append(jnp.dot(dlog, weight_out.T, preferred_element_type=jnp.float32))
    widths = [part.shape[1] for part in partials]
    joined = of_everyone(jnp.concatenate(partials, axis=1).astype(jnp.bfloat16), "tp")
    summed = jnp.split(joined, [sum(widths[:k]) for k in (1, 2, 3)], axis=1)
    grads_out = []
    grads_proj = []
    backs = []
    for band in range(4):
        dred = summed[band].astype(jnp.bfloat16)
        weight_in = projections[band][0]
        grads_out.append(
            jnp.dot(
                band_reduced[band].T, band_dlog[band], preferred_element_type=jnp.float32
            ).astype(jnp.bfloat16)[None]
        )
        rows_mine = lax.dynamic_slice_in_dim(band_rows[band], tp_index * own_width, own_width, 1)
        grads_proj.append(
            jnp.dot(rows_mine.T, dred, preferred_element_type=jnp.float32).astype(jnp.bfloat16)[
                None
            ]
        )
        weight_mine = lax.dynamic_slice_in_dim(weight_in, tp_index * own_width, own_width, 0)
        back = jnp.dot(dred, weight_mine.T, preferred_element_type=jnp.float32).astype(jnp.bfloat16)
        backs.append(back.reshape(groups, capacity, back.shape[1]))
    back_all = jnp.concatenate(backs, axis=1)
    returned = lax.all_to_all(back_all, "vocab", split_axis=0, concat_axis=0, tiled=True).reshape(
        tok_rows, back_all.shape[2]
    )
    tail_part = jnp.dot(dispatch_bf.T, returned, preferred_element_type=jnp.float32)
    grad_hidden = (head_mine + tail_part).astype(jnp.bfloat16)
    grads_cat = jnp.concatenate(
        [grad_words, jnp.pad(grad_clus, ((0, 0), (0, -clus_cols % 128)))], axis=1
    )
    head_sum = lax.psum_scatter(
        jnp.dot(hidden.T, grads_cat, preferred_element_type=jnp.float32).astype(jnp.bfloat16),
        "vocab",
        scatter_dimension=0,
        tiled=True,
    ).astype(jnp.float32)
    grad_head_words = head_sum[:, :word_cols].astype(jnp.bfloat16)
    grad_head_clusters = head_sum[:, word_cols : word_cols + clus_cols].astype(jnp.bfloat16)
    return (
        grad_hidden,
        grad_head_words,
        grad_head_clusters,
        grads_proj[0],
        grads_proj[1],
        grads_proj[2],
        grads_proj[3],
        grads_out[0],
        grads_out[1],
        grads_out[2],
        grads_out[3],
    )


def solution(mesh):
    return jax.shard_map(
        body,
        mesh=mesh,
        in_specs=(
            P("vocab", None),
            P("vocab", None),
            P("vocab"),
            P(None, "tp"),
            P(None, "tp"),
            P("vocab", None, None),
            P("vocab", None, None),
            P("vocab", None, None),
            P("vocab", None, None),
            P("vocab", None, "tp"),
            P("vocab", None, "tp"),
            P("vocab", None, "tp"),
            P("vocab", None, "tp"),
        ),
        out_specs=(
            P("vocab", "tp"),
            P("vocab", "tp"),
            P("vocab", "tp"),
            P("vocab", "tp", None),
            P("vocab", "tp", None),
            P("vocab", "tp", None),
            P("vocab", "tp", None),
            P("vocab", None, "tp"),
            P("vocab", None, "tp"),
            P("vocab", None, "tp"),
            P("vocab", None, "tp"),
        ),
        check_vma=False,
    )
```
